256 devices in a mesh: pair: 64 (over z, x, y_lo), mo: 4 (over y_hi, core).
Axes of the slice: x: 4, y: 4 (y_hi: 2, y_lo: 2; y = y_hi * 2 + y_lo), z: 8, core: 2. Of those that a mesh axis runs over, the one named last changes fastest.
Arguments:
- integrals: bfloat16 [1024, 1000, 1000], P('pair', 'mo'), may hold values from -6 to 6
- coeffs: bfloat16 [1000, 512], replicated, may hold values from -0.1875 to 0.1875
- mirror: int32 [1024], replicated, may hold values from 0 to 1023, as said below
Outputs:
- combined: float32 [1024, 512, 512], P(None, 'pair', 'mo')
The draws below stay inside these ranges and needn't reach their ends.
Inputs may be any that keep to these rules, and one draw needn't show every extreme that they name: mirror pairs the rows: mirror[mirror[k]] = k and mirror[k] != k for every row k; a row and its mirror may lie on any devices.
All inputs are finite; a program needn't handle non-finite values.
Results may differ from the reference program's by a relative error of at most 0.0029.
Values may be sent and summed in bfloat16 or wider, within the bound.
A program may use at most 128 MiB of HBM per device.

```python
import jax
import jax.numpy as jnp
from jax import lax

NBF = 1000
NMO = 512
ROWS = 1024


def draw_mirror(key, part):
    order = jax.random.permutation(key, ROWS).astype(jnp.int32)
    first = order[0::2]
    second = order[1::2]
    paired = jnp.zeros((ROWS,), jnp.int32).at[first].set(second)
    return paired.at[second].set(first)


def steps_of(stream_key, shape, pieces, smallest, high):
    def one(axis_at, blocks):
        heights = jax.random.uniform(jax.random.fold_in(jax.random.fold_in(stream_key, 6), axis_at), (blocks,), jnp.float32, smallest / len(pieces), high / len(pieces))
        return jnp.repeat(jnp.exp(heights), shape[axis_at] // blocks).reshape((-1,) + (1,) * (len(shape) - axis_at - 1))

    level = one(*pieces[0])
    for cut in pieces[1:]:
        level = level * one(*cut)
    return level


def centred(rng, shape, width, limit, split=(), held_as=jnp.bfloat16):
    values = width * jax.random.normal(rng, shape, jnp.float32)
    if split:
        values = values * steps_of(rng, shape, split, -0.22, 0.18)
    return jnp.clip(values, -limit, limit).astype(held_as)


def setup_inputs(seed: int = 0) -> dict:
    seeds = jax.random.split(jax.random.key(seed), 4)
    integrals = centred(seeds[0], (ROWS, NBF, NBF), 1.0, 6.0, ((0, 64), (1, 4)))
    coeffs = centred(seeds[1], (NBF, NMO), NBF ** -0.5, 0.1875)
    mirror = draw_mirror(jax.random.fold_in(seeds[3], 71), 0)
    return {"integrals": integrals, "coeffs": coeffs, "mirror": mirror}


def reference(integrals, coeffs, mirror):
    def one_row(block):
        quarter = jnp.dot(block, coeffs, preferred_element_type=jnp.float32).astype(jnp.bfloat16)
        return jnp.dot(coeffs.T, quarter, preferred_element_type=jnp.float32)

    half = lax.map(one_row, integrals)
    partner = jnp.take(half, mirror.astype(jnp.int32), axis=0)
    return 0.5 * (half + partner)
```

```python
import jax
import jax.numpy as jnp
from jax import lax
from jax.sharding import PartitionSpec as P


def make_on_device(n_pair, n_mo):
    def on_device(integrals, coeffs, mirror):
        rows, r_loc, nbf = integrals.shape
        nmo = coeffs.shape[1]
        c_j = coeffs.reshape(nbf, n_mo, nmo // n_mo).transpose(1, 0, 2)
        quarter = jnp.einsum(
            "krs,bsj->bkrj", integrals, c_j, preferred_element_type=jnp.float32
        ).astype(jnp.bfloat16)
        arrived = lax.all_to_all(quarter, "mo", 0, 0, tiled=True)
        c_r = coeffs.reshape(n_mo, r_loc, n_pair, nmo // n_pair)
        half = jnp.einsum(
            "brpi,bkrj->pkij", c_r, arrived, preferred_element_type=jnp.float32
        )
        pieces = lax.all_to_all(half.astype(jnp.bfloat16), "pair", 0, 0, tiled=True)
        pieces = pieces.reshape(n_pair * rows, nmo // n_pair, nmo // n_mo)
        pieces = pieces.astype(jnp.float32)
        partner = jnp.take(pieces, mirror, axis=0)
        return 0.5 * (pieces + partner)

    return on_device


def solution(mesh):
    return jax.shard_map(
        make_on_device(mesh.shape["pair"], mesh.shape["mo"]),
        mesh=mesh,
        in_specs=(P("pair", "mo", None), P(), P()),
        out_specs=P(None, "pair", "mo"),
        check_vma=False,
    )
```

```python
import jax
import jax.numpy as jnp
from jax import lax
from jax.experimental import pallas as pl
from jax.experimental.pallas import tpu as pltpu
from jax.sharding import PartitionSpec as P


def combine_kernel(mirror_ref, x_ref, o_ref):
    def body(k, carry):
        a = x_ref[k].astype(jnp.float32)
        b = x_ref[mirror_ref[k]].astype(jnp.float32)
        o_ref[k] = 0.5 * (a + b)
        return carry

    lax.fori_loop(0, x_ref.shape[0], body, 0, unroll=8)


def combine(pieces, mirror):
    return pl.pallas_call(
        combine_kernel,
        out_shape=jax.ShapeDtypeStruct(pieces.shape, jnp.float32),
        in_specs=[
            pl.BlockSpec(memory_space=pltpu.SMEM),
            pl.BlockSpec(memory_space=pltpu.VMEM),
        ],
        out_specs=pl.BlockSpec(memory_space=pltpu.VMEM),
    )(mirror, pieces)


def make_on_device(n_pair, n_mo):
    def on_device(integrals, coeffs, mirror):
        rows, r_loc, nbf = integrals.shape
        nmo = coeffs.shape[1]
        c_j = coeffs.reshape(nbf, n_mo, nmo // n_mo).transpose(1, 0, 2)
        quarter = jnp.einsum(
            "krs,bsj->bkrj", integrals, c_j, preferred_element_type=jnp.float32
        ).astype(jnp.bfloat16)
        arrived = lax.all_to_all(quarter, "mo", 0, 0, tiled=True)
        c_r = coeffs.reshape(n_mo, r_loc, n_pair, nmo // n_pair)
        half = jnp.einsum(
            "brpi,bkrj->pkij", c_r, arrived, preferred_element_type=jnp.float32
        )
        pieces = lax.all_to_all(half.astype(jnp.bfloat16), "pair", 0, 0, tiled=True)
        pieces = pieces.reshape(n_pair * rows, nmo // n_pair, nmo // n_mo)
        return combine(pieces, mirror)

    return on_device


def solution(mesh):
    return jax.shard_map(
        make_on_device(mesh.shape["pair"], mesh.shape["mo"]),
        mesh=mesh,
        in_specs=(P("pair", "mo", None), P(), P()),
        out_specs=P(None, "pair", "mo"),
        check_vma=False,
    )
```

```python
import jax
import jax.numpy as jnp
from jax import lax
from jax.experimental import pallas as pl
from jax.experimental.pallas import tpu as pltpu
from jax.sharding import PartitionSpec as P

N_CHUNK = 4


def combine_kernel(mirror_ref, *refs):
    xs, o_ref = refs[:-1], refs[-1]
    n_src, kc = xs[0].shape[0], xs[0].shape[1]
    rows = kc * len(xs)

    def body(src, carry):
        for c, x in enumerate(xs):
            for kk in range(kc):
                k = src * rows + c * kc + kk
                m = mirror_ref[k]
                ms, mc, mk = m // rows, (m % rows) // kc, m % kc
                b = xs[0][ms, mk]
                for c2 in range(1, len(xs)):
                    b = jnp.where(mc == c2, xs[c2][ms, mk], b)
                a = x[src, kk].astype(jnp.float32)
                o_ref[k] = 0.5 * (a + b.astype(jnp.float32))
        return carry

    lax.fori_loop(0, n_src, body, 0)


def combine(chunks, mirror):
    n_src, kc, a, b = chunks[0].shape
    return pl.pallas_call(
        combine_kernel,
        out_shape=jax.ShapeDtypeStruct((n_src * kc * len(chunks), a, b), jnp.float32),
        in_specs=[pl.BlockSpec(memory_space=pltpu.SMEM)]
        + [pl.BlockSpec(memory_space=pltpu.VMEM)] * len(chunks),
        out_specs=pl.BlockSpec(memory_space=pltpu.VMEM),
    )(mirror, *chunks)


def make_on_device(n_pair, n_mo):
    def on_device(integrals, coeffs, mirror):
        rows, r_loc, nbf = integrals.shape
        nmo = coeffs.shape[1]
        kc = rows // N_CHUNK
        c_j = coeffs.reshape(nbf, n_mo, nmo // n_mo).transpose(1, 0, 2)
        c_r = coeffs.reshape(n_mo, r_loc, n_pair, nmo // n_pair)
        outs = []
        me = lax.axis_index("mo")
        for c in range(N_CHUNK):
            block = integrals[c * kc:(c + 1) * kc]
            quarter = jnp.einsum(
                "krs,bsj->bkrj", block, c_j, preferred_element_type=jnp.float32
            ).astype(jnp.bfloat16)
            half = None
            for s in range(n_mo):
                dst = lax.rem(me + s, n_mo)
                src = lax.rem(me + n_mo - s, n_mo)
                piece = lax.dynamic_index_in_dim(quarter, dst, 0, keepdims=False)
                if s:
                    perm = [(i, (i + s) % n_mo) for i in range(n_mo)]
                    piece = lax.ppermute(piece, "mo", perm)
                coef = lax.dynamic_index_in_dim(c_r, src, 0, keepdims=False)
                term = jnp.einsum(
                    "rpi,krj->pkij", coef, piece, preferred_element_type=jnp.float32
                )
                half = term if half is None else half + term
            outs.append(lax.all_to_all(half.astype(jnp.bfloat16), "pair", 0, 0, tiled=True))
        return combine(outs, mirror)

    return on_device


def solution(mesh):
    return jax.shard_map(
        make_on_device(mesh.shape["pair"], mesh.shape["mo"]),
        mesh=mesh,
        in_specs=(P("pair", "mo", None), P(), P()),
        out_specs=P(None, "pair", "mo"),
        check_vma=False,
    )
```

```python
import functools

import jax
import jax.numpy as jnp
from jax import lax
from jax.experimental import pallas as pl
from jax.experimental.pallas import tpu as pltpu
from jax.sharding import PartitionSpec as P

MESH = pl.DeviceIdType.MESH


def exchange_combine_kernel(n_pair, mirror_ref, x_ref, o_ref, held, send_sems, recv_sems, own_sem):
    me = lax.axis_index("pair")
    mo = lax.axis_index("mo")
    rows = x_ref.shape[1]

    def peer(s):
        return lax.rem(me + s, n_pair)

    barrier = pltpu.get_barrier_semaphore()

    def greet(s, carry):
        pl.semaphore_signal(barrier, 1, device_id=(peer(s), mo), device_id_type=MESH)
        return carry

    lax.fori_loop(1, n_pair, greet, 0)
    pl.semaphore_wait(barrier, n_pair - 1)

    own = pltpu.make_async_copy(x_ref.at[me], held.at[me], own_sem)
    own.start()

    def send(s):
        return pltpu.make_async_remote_copy(
            src_ref=x_ref.at[peer(s)],
            dst_ref=held.at[me],
            send_sem=send_sems.at[s],
            recv_sem=recv_sems.at[s],
            device_id=(peer(s), mo),
            device_id_type=MESH,
        )

    def start(s, carry):
        send(s).start()
        return carry

    def finish(s, carry):
        send(s).wait()
        return carry

    lax.fori_loop(1, n_pair, start, 0)
    own.wait()
    lax.fori_loop(1, n_pair, finish, 0)

    def body(src, carry):
        for kk in range(rows):
            k = src * rows + kk
            m = mirror_ref[k]
            a = held[src, kk].astype(jnp.float32)
            b = held[m // rows, m % rows].astype(jnp.float32)
            o_ref[k] = 0.5 * (a + b)
        return carry

    lax.fori_loop(0, n_pair, body, 0)


def exchange_combine(half, mirror, n_pair):
    _, rows, a, b = half.shape
    return pl.pallas_call(
        functools.partial(exchange_combine_kernel, n_pair),
        out_shape=jax.ShapeDtypeStruct((n_pair * rows, a, b), jnp.float32),
        in_specs=[
            pl.BlockSpec(memory_space=pltpu.SMEM),
            pl.BlockSpec(memory_space=pltpu.VMEM),
        ],
        out_specs=pl.BlockSpec(memory_space=pltpu.VMEM),
        scratch_shapes=[
            pltpu.VMEM(half.shape, half.dtype),
            pltpu.SemaphoreType.DMA((n_pair,)),
            pltpu.SemaphoreType.DMA((n_pair,)),
            pltpu.SemaphoreType.DMA(()),
        ],
        compiler_params=pltpu.CompilerParams(collective_id=0, has_side_effects=True),
    )(mirror, half)


def make_on_device(n_pair, n_mo):
    def on_device(integrals, coeffs, mirror):
        rows, r_loc, nbf = integrals.shape
        nmo = coeffs.shape[1]
        c_j = coeffs.reshape(nbf, n_mo, nmo // n_mo).transpose(1, 0, 2)
        quarter = jnp.einsum(
            "krs,bsj->bkrj", integrals, c_j, preferred_element_type=jnp.float32
        ).astype(jnp.bfloat16)
        arrived = lax.all_to_all(quarter, "mo", 0, 0, tiled=True)
        c_r = coeffs.reshape(n_mo, r_loc, n_pair, nmo // n_pair)
        half = jnp.einsum(
            "brpi,bkrj->pkij", c_r, arrived, preferred_element_type=jnp.float32
        )
        return exchange_combine(half.astype(jnp.bfloat16), mirror, n_pair)

    return on_device


def solution(mesh):
    return jax.shard_map(
        make_on_device(mesh.shape["pair"], mesh.shape["mo"]),
        mesh=mesh,
        in_specs=(P("pair", "mo", None), P(), P()),
        out_specs=P(None, "pair", "mo"),
        check_vma=False,
    )
```

```python
import functools

import jax
import jax.numpy as jnp
from jax import lax
from jax.experimental import pallas as pl
from jax.experimental.pallas import tpu as pltpu
from jax.sharding import PartitionSpec as P

MESH = pl.DeviceIdType.MESH
N_CHUNK = 4


def fused_kernel(n_pair, n_mo, n_chunk, mirror_ref, q_ref, ct_ref, o_ref,
                 arrived, sendbuf, held, mo_send, mo_recv, pr_send, pr_recv, own_sem):
    me = lax.axis_index("pair")
    mo = lax.axis_index("mo")
    rows = q_ref.shape[1]
    kc = rows // n_chunk

    def chunk(c):
        return pl.ds(c * kc, kc)

    def mo_copy(c, s):
        b = lax.rem(mo + s, n_mo)
        return pltpu.make_async_remote_copy(
            src_ref=q_ref.at[b, chunk(c)],
            dst_ref=arrived.at[mo, chunk(c)],
            send_sem=mo_send.at[c, s],
            recv_sem=mo_recv.at[c, s],
            device_id=(me, b),
            device_id_type=MESH,
        )

    def pair_copy(c, s):
        p = lax.rem(me + s, n_pair)
        return pltpu.make_async_remote_copy(
            src_ref=sendbuf.at[chunk(c), p],
            dst_ref=held.at[me, chunk(c)],
            send_sem=pr_send.at[c, s],
            recv_sem=pr_recv.at[c, s],
            device_id=(p, mo),
            device_id_type=MESH,
        )

    def own_mo(c):
        return pltpu.make_async_copy(q_ref.at[mo, chunk(c)], arrived.at[mo, chunk(c)], own_sem.at[0, c])

    def own_pair(c):
        return pltpu.make_async_copy(sendbuf.at[chunk(c), me], held.at[me, chunk(c)], own_sem.at[1, c])

    barrier = pltpu.get_barrier_semaphore()

    def greet(s, carry):
        pl.semaphore_signal(barrier, 1, device_id=(lax.rem(me + s, n_pair), mo), device_id_type=MESH)
        return carry

    lax.fori_loop(1, n_pair, greet, 0)
    for s in range(1, n_mo):
        pl.semaphore_signal(barrier, 1, device_id=(me, lax.rem(mo + s, n_mo)), device_id_type=MESH)
    pl.semaphore_wait(barrier, n_pair - 1 + n_mo - 1)

    for c in range(n_chunk):
        own_mo(c).start()
        for s in range(1, n_mo):
            mo_copy(c, s).start()

    for c in range(n_chunk):
        own_mo(c).wait()
        for s in range(1, n_mo):
            mo_copy(c, s).wait()

        def transform(t, carry):
            k = c * kc + t
            acc = jnp.dot(ct_ref[0], arrived[0, k], preferred_element_type=jnp.float32)
            for b in range(1, n_mo):
                acc += jnp.dot(ct_ref[b], arrived[b, k], preferred_element_type=jnp.float32)
            sendbuf[k] = acc.reshape(n_pair, -1, acc.shape[-1]).astype(sendbuf.dtype)
            return carry

        lax.fori_loop(0, kc, transform, 0)
        own_pair(c).start()

        def start(s, carry):
            pair_copy(c, s).start()
            return carry

        lax.fori_loop(1, n_pair, start, 0)

    for c in range(n_chunk):
        own_pair(c).wait()

        def finish(s, carry):
            pair_copy(c, s).wait()
            return carry

        lax.fori_loop(1, n_pair, finish, 0)

    def combine(src, carry):
        for kk in range(rows):
            k = src * rows + kk
            m = mirror_ref[k]
            a = held[src, kk].astype(jnp.float32)
            b = held[m // rows, m % rows].astype(jnp.float32)
            o_ref[k] = 0.5 * (a + b)
        return carry

    lax.fori_loop(0, n_pair, combine, 0)


def fused(quarter, ct, mirror, n_pair):
    n_mo, rows, r_loc, jw = quarter.shape
    nmo = ct.shape[1]
    iw = nmo // n_pair
    return pl.pallas_call(
        functools.partial(fused_kernel, n_pair, n_mo, N_CHUNK),
        out_shape=jax.ShapeDtypeStruct((n_pair * rows, iw, jw), jnp.float32),
        in_specs=[
            pl.BlockSpec(memory_space=pltpu.SMEM),
            pl.BlockSpec(memory_space=pltpu.VMEM),
            pl.BlockSpec(memory_space=pltpu.VMEM),
        ],
        out_specs=pl.BlockSpec(memory_space=pltpu.VMEM),
        scratch_shapes=[
            pltpu.VMEM(quarter.shape, quarter.dtype),
            pltpu.VMEM((rows, n_pair, iw, jw), jnp.bfloat16),
            pltpu.VMEM((n_pair, rows, iw, jw), jnp.bfloat16),
            pltpu.SemaphoreType.DMA((N_CHUNK, n_mo)),
            pltpu.SemaphoreType.DMA((N_CHUNK, n_mo)),
            pltpu.SemaphoreType.DMA((N_CHUNK, n_pair)),
            pltpu.SemaphoreType.DMA((N_CHUNK, n_pair)),
            pltpu.SemaphoreType.DMA((2, N_CHUNK)),
        ],
        compiler_params=pltpu.CompilerParams(
            collective_id=0, has_side_effects=True, vmem_limit_bytes=48 * 1024 * 1024
        ),
    )(mirror, quarter, ct)


def make_on_device(n_pair, n_mo):
    def on_device(integrals, coeffs, mirror):
        rows, r_loc, nbf = integrals.shape
        nmo = coeffs.shape[1]
        c_j = coeffs.reshape(nbf, n_mo, nmo // n_mo).transpose(1, 0, 2)
        quarter = jnp.einsum(
            "krs,bsj->bkrj", integrals, c_j, preferred_element_type=jnp.float32
        ).astype(jnp.bfloat16)
        ct = coeffs.reshape(n_mo, r_loc, nmo).transpose(0, 2, 1)
        return fused(quarter, ct, mirror, n_pair)

    return on_device


def solution(mesh):
    return jax.shard_map(
        make_on_device(mesh.shape["pair"], mesh.shape["mo"]),
        mesh=mesh,
        in_specs=(P("pair", "mo", None), P(), P()),
        out_specs=P(None, "pair", "mo"),
        check_vma=False,
    )
```

```python
import functools

import jax
import jax.numpy as jnp
from jax import lax
from jax.experimental import pallas as pl
from jax.experimental.pallas import tpu as pltpu
from jax.sharding import PartitionSpec as P

MESH = pl.DeviceIdType.MESH
N_CHUNK = 8


def fused_kernel(n_pair, n_mo, n_chunk, mirror_ref, q_ref, ct_ref, o_ref,
                 arrived, sendbuf, held, mo_send, mo_recv, pr_send, pr_recv, own_sem):
    me = lax.axis_index("pair")
    mo = lax.axis_index("mo")
    rows = q_ref.shape[1]
    kc = rows // n_chunk

    def chunk(c):
        return pl.ds(c * kc, kc)

    def mo_copy(c, s):
        b = lax.rem(mo + s, n_mo)
        return pltpu.make_async_remote_copy(
            src_ref=q_ref.at[b, chunk(c)],
            dst_ref=arrived.at[mo, chunk(c)],
            send_sem=mo_send.at[c, s],
            recv_sem=mo_recv.at[c, s],
            device_id=(me, b),
            device_id_type=MESH,
        )

    def pair_copy(c, s):
        p = lax.rem(me + s, n_pair)
        return pltpu.make_async_remote_copy(
            src_ref=sendbuf.at[chunk(c), p],
            dst_ref=held.at[me, chunk(c)],
            send_sem=pr_send.at[c, s],
            recv_sem=pr_recv.at[c, s],
            device_id=(p, mo),
            device_id_type=MESH,
        )

    def own_mo(c):
        return pltpu.make_async_copy(q_ref.at[mo, chunk(c)], arrived.at[mo, chunk(c)], own_sem.at[0, c])

    def own_pair(c):
        return pltpu.make_async_copy(sendbuf.at[chunk(c), me], held.at[me, chunk(c)], own_sem.at[1, c])

    barrier = pltpu.get_barrier_semaphore()

    def greet(s, carry):
        pl.semaphore_signal(barrier, 1, device_id=(lax.rem(me + s, n_pair), mo), device_id_type=MESH)
        return carry

    lax.fori_loop(1, n_pair, greet, 0)
    for s in range(1, n_mo):
        pl.semaphore_signal(barrier, 1, device_id=(me, lax.rem(mo + s, n_mo)), device_id_type=MESH)
    pl.semaphore_wait(barrier, n_pair - 1 + n_mo - 1)

    for c in range(n_chunk):
        own_mo(c).start()
        for s in range(1, n_mo):
            mo_copy(c, s).start()

    for c in range(n_chunk):
        own_mo(c).wait()
        for s in range(1, n_mo):
            mo_copy(c, s).wait()

        def transform(t, carry):
            k = c * kc + t
            acc = jnp.dot(ct_ref[0], arrived[0, k], preferred_element_type=jnp.float32)
            for b in range(1, n_mo):
                acc += jnp.dot(ct_ref[b], arrived[b, k], preferred_element_type=jnp.float32)
            sendbuf[k] = acc.reshape(n_pair, -1, acc.shape[-1]).astype(sendbuf.dtype)
            return carry

        lax.fori_loop(0, kc, transform, 0)
        own_pair(c).start()

        def start(s, carry):
            pair_copy(c, s).start()
            return carry

        lax.fori_loop(1, n_pair, start, 0)

    for c in range(n_chunk):
        own_pair(c).wait()

        def finish(s, carry):
            pair_copy(c, s).wait()
            return carry

        lax.fori_loop(1, n_pair, finish, 0)

    def combine(src, carry):
        for kk in range(rows):
            k = src * rows + kk
            m = mirror_ref[k]
            a = held[src, kk].astype(jnp.float32)
            b = held[m // rows, m % rows].astype(jnp.float32)
            o_ref[k] = 0.5 * (a + b)
        return carry

    lax.fori_loop(0, n_pair, combine, 0)


def fused(quarter, ct, mirror, n_pair):
    n_mo, rows, r_loc, jw = quarter.shape
    nmo = ct.shape[1]
    iw = nmo // n_pair
    return pl.pallas_call(
        functools.partial(fused_kernel, n_pair, n_mo, N_CHUNK),
        out_shape=jax.ShapeDtypeStruct((n_pair * rows, iw, jw), jnp.float32),
        in_specs=[
            pl.BlockSpec(memory_space=pltpu.SMEM),
            pl.BlockSpec(memory_space=pltpu.VMEM),
            pl.BlockSpec(memory_space=pltpu.VMEM),
        ],
        out_specs=pl.BlockSpec(memory_space=pltpu.VMEM),
        scratch_shapes=[
            pltpu.VMEM(quarter.shape, quarter.dtype),
            pltpu.VMEM((rows, n_pair, iw, jw), jnp.bfloat16),
            pltpu.VMEM((n_pair, rows, iw, jw), jnp.bfloat16),
            pltpu.SemaphoreType.DMA((N_CHUNK, n_mo)),
            pltpu.SemaphoreType.DMA((N_CHUNK, n_mo)),
            pltpu.SemaphoreType.DMA((N_CHUNK, n_pair)),
            pltpu.SemaphoreType.DMA((N_CHUNK, n_pair)),
            pltpu.SemaphoreType.DMA((2, N_CHUNK)),
        ],
        compiler_params=pltpu.CompilerParams(
            collective_id=0, has_side_effects=True, vmem_limit_bytes=48 * 1024 * 1024
        ),
    )(mirror, quarter, ct)


def make_on_device(n_pair, n_mo):
    def on_device(integrals, coeffs, mirror):
        rows, r_loc, nbf = integrals.shape
        nmo = coeffs.shape[1]
        c_j = coeffs.reshape(nbf, n_mo, nmo // n_mo).transpose(1, 0, 2)
        quarter = jnp.einsum(
            "krs,bsj->bkrj", integrals, c_j, preferred_element_type=jnp.float32
        ).astype(jnp.bfloat16)
        ct = coeffs.reshape(n_mo, r_loc, nmo).transpose(0, 2, 1)
        return fused(quarter, ct, mirror, n_pair)

    return on_device


def solution(mesh):
    return jax.shard_map(
        make_on_device(mesh.shape["pair"], mesh.shape["mo"]),
        mesh=mesh,
        in_specs=(P("pair", "mo", None), P(), P()),
        out_specs=P(None, "pair", "mo"),
        check_vma=False,
    )
```

```python
import functools

import jax
import jax.numpy as jnp
from jax import lax
from jax.experimental import pallas as pl
from jax.experimental.pallas import tpu as pltpu
from jax.sharding import PartitionSpec as P

MESH = pl.DeviceIdType.MESH
N_CHUNK = 4


def fused_kernel(n_pair, n_mo, n_chunk, mirror_ref, x_ref, c_ref, ct_ref, o_ref,
                 q_ref, arrived, sendbuf, held, mo_send, mo_recv, pr_send, pr_recv, own_sem):
    me = lax.axis_index("pair")
    mo = lax.axis_index("mo")
    rows = q_ref.shape[1]
    kc = rows // n_chunk

    def chunk(c):
        return pl.ds(c * kc, kc)

    def mo_copy(c, s):
        b = lax.rem(mo + s, n_mo)
        return pltpu.make_async_remote_copy(
            src_ref=q_ref.at[b, chunk(c)],
            dst_ref=arrived.at[mo, chunk(c)],
            send_sem=mo_send.at[c, s],
            recv_sem=mo_recv.at[c, s],
            device_id=(me, b),
            device_id_type=MESH,
        )

    def pair_copy(c, s):
        p = lax.rem(me + s, n_pair)
        return pltpu.make_async_remote_copy(
            src_ref=sendbuf.at[chunk(c), p],
            dst_ref=held.at[me, chunk(c)],
            send_sem=pr_send.at[c, s],
            recv_sem=pr_recv.at[c, s],
            device_id=(p, mo),
            device_id_type=MESH,
        )

    def own_mo(c):
        return pltpu.make_async_copy(q_ref.at[mo, chunk(c)], arrived.at[mo, chunk(c)], own_sem.at[0, c])

    def own_pair(c):
        return pltpu.make_async_copy(sendbuf.at[chunk(c), me], held.at[me, chunk(c)], own_sem.at[1, c])

    barrier = pltpu.get_barrier_semaphore()

    def greet(s, carry):
        pl.semaphore_signal(barrier, 1, device_id=(lax.rem(me + s, n_pair), mo), device_id_type=MESH)
        return carry

    lax.fori_loop(1, n_pair, greet, 0)
    for s in range(1, n_mo):
        pl.semaphore_signal(barrier, 1, device_id=(me, lax.rem(mo + s, n_mo)), device_id_type=MESH)
    pl.semaphore_wait(barrier, n_pair - 1 + n_mo - 1)

    jw = q_ref.shape[-1]
    for c in range(n_chunk):

        def first(t, carry):
            k = c * kc + t
            res = jnp.dot(x_ref[k], c_ref[...], preferred_element_type=jnp.float32)
            res = res.astype(q_ref.dtype)
            for b in range(n_mo):
                q_ref[b, k] = res[:, b * jw:(b + 1) * jw]
            return carry

        lax.fori_loop(0, kc, first, 0)
        own_mo(c).start()
        for s in range(1, n_mo):
            mo_copy(c, s).start()

    for c in range(n_chunk):
        own_mo(c).wait()
        for s in range(1, n_mo):
            mo_copy(c, s).wait()

        def transform(t, carry):
            k = c * kc + t
            acc = jnp.dot(ct_ref[0], arrived[0, k], preferred_element_type=jnp.float32)
            for b in range(1, n_mo):
                acc += jnp.dot(ct_ref[b], arrived[b, k], preferred_element_type=jnp.float32)
            sendbuf[k] = acc.reshape(n_pair, -1, acc.shape[-1]).astype(sendbuf.dtype)
            return carry

        lax.fori_loop(0, kc, transform, 0)
        own_pair(c).start()

        def start(s, carry):
            pair_copy(c, s).start()
            return carry

        lax.fori_loop(1, n_pair, start, 0)

    for c in range(n_chunk):
        own_pair(c).wait()

        def finish(s, carry):
            pair_copy(c, s).wait()
            return carry

        lax.fori_loop(1, n_pair, finish, 0)

    def combine(src, carry):
        for kk in range(rows):
            k = src * rows + kk
            m = mirror_ref[k]
            a = held[src, kk].astype(jnp.float32)
            b = held[m // rows, m % rows].astype(jnp.float32)
            o_ref[k] = 0.5 * (a + b)
        return carry

    lax.fori_loop(0, n_pair, combine, 0)


def fused(integrals, coeffs, ct, mirror, n_pair, n_mo):
    rows, r_loc, _ = integrals.shape
    nmo = coeffs.shape[1]
    iw, jw = nmo // n_pair, nmo // n_mo
    return pl.pallas_call(
        functools.partial(fused_kernel, n_pair, n_mo, N_CHUNK),
        out_shape=jax.ShapeDtypeStruct((n_pair * rows, iw, jw), jnp.float32),
        in_specs=[pl.BlockSpec(memory_space=pltpu.SMEM)]
        + [pl.BlockSpec(memory_space=pltpu.VMEM)] * 3,
        out_specs=pl.BlockSpec(memory_space=pltpu.VMEM),
        scratch_shapes=[
            pltpu.VMEM((n_mo, rows, r_loc, jw), jnp.bfloat16),
            pltpu.VMEM((n_mo, rows, r_loc, jw), jnp.bfloat16),
            pltpu.VMEM((rows, n_pair, iw, jw), jnp.bfloat16),
            pltpu.VMEM((n_pair, rows, iw, jw), jnp.bfloat16),
            pltpu.SemaphoreType.DMA((N_CHUNK, n_mo)),
            pltpu.SemaphoreType.DMA((N_CHUNK, n_mo)),
            pltpu.SemaphoreType.DMA((N_CHUNK, n_pair)),
            pltpu.SemaphoreType.DMA((N_CHUNK, n_pair)),
            pltpu.SemaphoreType.DMA((2, N_CHUNK)),
        ],
        compiler_params=pltpu.CompilerParams(
            collective_id=0, has_side_effects=True, vmem_limit_bytes=60 * 1024 * 1024
        ),
    )(mirror, integrals, coeffs, ct)


def make_on_device(n_pair, n_mo):
    def on_device(integrals, coeffs, mirror):
        rows, r_loc, nbf = integrals.shape
        nmo = coeffs.shape[1]
        ct = coeffs.reshape(n_mo, r_loc, nmo).transpose(0, 2, 1)
        return fused(integrals, coeffs, ct, mirror, n_pair, n_mo)

    return on_device


def solution(mesh):
    return jax.shard_map(
        make_on_device(mesh.shape["pair"], mesh.shape["mo"]),
        mesh=mesh,
        in_specs=(P("pair", "mo", None), P(), P()),
        out_specs=P(None, "pair", "mo"),
        check_vma=False,
    )
```

```python
import functools

import jax
import jax.numpy as jnp
from jax import lax
from jax.experimental import pallas as pl
from jax.experimental.pallas import tpu as pltpu
from jax.sharding import PartitionSpec as P

MESH = pl.DeviceIdType.MESH
N_CHUNK = 4


def fused_kernel(n_pair, n_mo, n_chunk, mirror_ref, q_ref, ct_ref, o_ref,
                 arrived, sendbuf, held, mo_send, mo_recv, pr_send, pr_recv, own_sem):
    me = lax.axis_index("pair")
    mo = lax.axis_index("mo")
    rows = q_ref.shape[1]
    kc = rows // n_chunk

    def chunk(c):
        return pl.ds(c * kc, kc)

    def mo_copy(c, s):
        b = lax.rem(mo + s, n_mo)
        return pltpu.make_async_remote_copy(
            src_ref=q_ref.at[b, chunk(c)],
            dst_ref=arrived.at[chunk(c), mo],
            send_sem=mo_send.at[c, s],
            recv_sem=mo_recv.at[c, s],
            device_id=(me, b),
            device_id_type=MESH,
        )

    def pair_copy(c, s):
        p = lax.rem(me + s, n_pair)
        return pltpu.make_async_remote_copy(
            src_ref=sendbuf.at[chunk(c), p],
            dst_ref=held.at[me, chunk(c)],
            send_sem=pr_send.at[c, s],
            recv_sem=pr_recv.at[c, s],
            device_id=(p, mo),
            device_id_type=MESH,
        )

    def own_mo(c):
        return pltpu.make_async_copy(q_ref.at[mo, chunk(c)], arrived.at[chunk(c), mo], own_sem.at[0, c])

    def own_pair(c):
        return pltpu.make_async_copy(sendbuf.at[chunk(c), me], held.at[me, chunk(c)], own_sem.at[1, c])

    barrier = pltpu.get_barrier_semaphore()

    def greet(s, carry):
        pl.semaphore_signal(barrier, 1, device_id=(lax.rem(me + s, n_pair), mo), device_id_type=MESH)
        return carry

    lax.fori_loop(1, n_pair, greet, 0)
    for s in range(1, n_mo):
        pl.semaphore_signal(barrier, 1, device_id=(me, lax.rem(mo + s, n_mo)), device_id_type=MESH)
    pl.semaphore_wait(barrier, n_pair - 1 + n_mo - 1)

    for c in range(n_chunk):
        own_mo(c).start()
        for s in range(1, n_mo):
            mo_copy(c, s).start()

    for c in range(n_chunk):
        own_mo(c).wait()
        for s in range(1, n_mo):
            mo_copy(c, s).wait()

        def transform(t, carry):
            k = c * kc + t
            block = arrived[k]
            block = block.reshape(-1, block.shape[-1])
            acc = jnp.dot(ct_ref[...], block, preferred_element_type=jnp.float32)
            sendbuf[k] = acc.reshape(n_pair, -1, acc.shape[-1]).astype(sendbuf.dtype)
            return carry

        lax.fori_loop(0, kc, transform, 0)
        own_pair(c).start()

        def start(s, carry):
            pair_copy(c, s).start()
            return carry

        lax.fori_loop(1, n_pair, start, 0)

    for c in range(n_chunk):
        own_pair(c).wait()

        def finish(s, carry):
            pair_copy(c, s).wait()
            return carry

        lax.fori_loop(1, n_pair, finish, 0)

    def combine(src, carry):
        for kk in range(rows):
            k = src * rows + kk
            m = mirror_ref[k]
            a = held[src, kk].astype(jnp.float32)
            b = held[m // rows, m % rows].astype(jnp.float32)
            o_ref[k] = 0.5 * (a + b)
        return carry

    lax.fori_loop(0, n_pair, combine, 0)


def fused(quarter, coeffs, mirror, n_pair):
    n_mo, rows, r_loc, jw = quarter.shape
    nmo = coeffs.shape[1]
    iw = nmo // n_pair
    r_pad = -(-r_loc // 16) * 16
    quarter = jnp.pad(quarter, ((0, 0), (0, 0), (0, r_pad - r_loc), (0, 0)))
    ct = coeffs.reshape(n_mo, r_loc, nmo)
    ct = jnp.pad(ct, ((0, 0), (0, r_pad - r_loc), (0, 0))).reshape(n_mo * r_pad, nmo).T
    return pl.pallas_call(
        functools.partial(fused_kernel, n_pair, n_mo, N_CHUNK),
        out_shape=jax.ShapeDtypeStruct((n_pair * rows, iw, jw), jnp.float32),
        in_specs=[
            pl.BlockSpec(memory_space=pltpu.SMEM),
            pl.BlockSpec(memory_space=pltpu.VMEM),
            pl.BlockSpec(memory_space=pltpu.VMEM),
        ],
        out_specs=pl.BlockSpec(memory_space=pltpu.VMEM),
        scratch_shapes=[
            pltpu.VMEM((rows, n_mo, r_pad, jw), quarter.dtype),
            pltpu.VMEM((rows, n_pair, iw, jw), jnp.bfloat16),
            pltpu.VMEM((n_pair, rows, iw, jw), jnp.bfloat16),
            pltpu.SemaphoreType.DMA((N_CHUNK, n_mo)),
            pltpu.SemaphoreType.DMA((N_CHUNK, n_mo)),
            pltpu.SemaphoreType.DMA((N_CHUNK, n_pair)),
            pltpu.SemaphoreType.DMA((N_CHUNK, n_pair)),
            pltpu.SemaphoreType.DMA((2, N_CHUNK)),
        ],
        compiler_params=pltpu.CompilerParams(
            collective_id=0, has_side_effects=True, vmem_limit_bytes=48 * 1024 * 1024
        ),
    )(mirror, quarter, ct)


def make_on_device(n_pair, n_mo):
    def on_device(integrals, coeffs, mirror):
        rows, r_loc, nbf = integrals.shape
        nmo = coeffs.shape[1]
        c_j = coeffs.reshape(nbf, n_mo, nmo // n_mo).transpose(1, 0, 2)
        quarter = jnp.einsum(
            "krs,bsj->bkrj", integrals, c_j, preferred_element_type=jnp.float32
        ).astype(jnp.bfloat16)
        return fused(quarter, coeffs, mirror, n_pair)

    return on_device


def solution(mesh):
    return jax.shard_map(
        make_on_device(mesh.shape["pair"], mesh.shape["mo"]),
        mesh=mesh,
        in_specs=(P("pair", "mo", None), P(), P()),
        out_specs=P(None, "pair", "mo"),
        check_vma=False,
    )
```

```python
import functools

import jax
import jax.numpy as jnp
from jax import lax
from jax.experimental import pallas as pl
from jax.experimental.pallas import tpu as pltpu
from jax.sharding import PartitionSpec as P

MESH = pl.DeviceIdType.MESH
N_CHUNK = 4
MO_AHEAD = 2


def fused_kernel(n_pair, n_mo, n_chunk, mirror_ref, q_ref, ct_ref, o_ref,
                 arrived, sendbuf, held, mo_send, mo_recv, pr_send, pr_recv, own_sem):
    me = lax.axis_index("pair")
    mo = lax.axis_index("mo")
    rows = q_ref.shape[1]
    kc = rows // n_chunk

    def chunk(c):
        return pl.ds(c * kc, kc)

    def mo_copy(c, s):
        b = lax.rem(mo + s, n_mo)
        return pltpu.make_async_remote_copy(
            src_ref=q_ref.at[b, chunk(c)],
            dst_ref=arrived.at[chunk(c), mo],
            send_sem=mo_send.at[c, s],
            recv_sem=mo_recv.at[c, s],
            device_id=(me, b),
            device_id_type=MESH,
        )

    def pair_copy(c, s):
        p = lax.rem(me + s, n_pair)
        return pltpu.make_async_remote_copy(
            src_ref=sendbuf.at[chunk(c), p],
            dst_ref=held.at[me, chunk(c)],
            send_sem=pr_send.at[c, s],
            recv_sem=pr_recv.at[c, s],
            device_id=(p, mo),
            device_id_type=MESH,
        )

    def own_mo(c):
        return pltpu.make_async_copy(q_ref.at[mo, chunk(c)], arrived.at[chunk(c), mo], own_sem.at[0, c])

    def own_pair(c):
        return pltpu.make_async_copy(sendbuf.at[chunk(c), me], held.at[me, chunk(c)], own_sem.at[1, c])

    barrier = pltpu.get_barrier_semaphore()

    def greet(s, carry):
        pl.semaphore_signal(barrier, 1, device_id=(lax.rem(me + s, n_pair), mo), device_id_type=MESH)
        return carry

    lax.fori_loop(1, n_pair, greet, 0)
    for s in range(1, n_mo):
        pl.semaphore_signal(barrier, 1, device_id=(me, lax.rem(mo + s, n_mo)), device_id_type=MESH)
    pl.semaphore_wait(barrier, n_pair - 1 + n_mo - 1)

    def start_mo(c):
        own_mo(c).start()
        for s in range(1, n_mo):
            mo_copy(c, s).start()

    for c in range(min(MO_AHEAD, n_chunk)):
        start_mo(c)

    for c in range(n_chunk):
        own_mo(c).wait()
        for s in range(1, n_mo):
            mo_copy(c, s).wait()

        def transform(t, carry):
            k = c * kc + t
            block = arrived[k]
            block = block.reshape(-1, block.shape[-1])
            acc = jnp.dot(ct_ref[...], block, preferred_element_type=jnp.float32)
            sendbuf[k] = acc.reshape(n_pair, -1, acc.shape[-1]).astype(sendbuf.dtype)
            return carry

        lax.fori_loop(0, kc, transform, 0)
        own_pair(c).start()

        def start(s, carry):
            pair_copy(c, s).start()
            return carry

        lax.fori_loop(1, n_pair, start, 0)
        if c + MO_AHEAD < n_chunk:
            start_mo(c + MO_AHEAD)

    for c in range(n_chunk):
        own_pair(c).wait()

        def finish(s, carry):
            pair_copy(c, s).wait()
            return carry

        lax.fori_loop(1, n_pair, finish, 0)

    def combine(src, carry):
        for kk in range(rows):
            k = src * rows + kk
            m = mirror_ref[k]
            a = held[src, kk].astype(jnp.float32)
            b = held[m // rows, m % rows].astype(jnp.float32)
            o_ref[k] = 0.5 * (a + b)
        return carry

    lax.fori_loop(0, n_pair, combine, 0)


def fused(quarter, coeffs, mirror, n_pair):
    n_mo, rows, r_loc, jw = quarter.shape
    nmo = coeffs.shape[1]
    iw = nmo // n_pair
    r_pad = -(-r_loc // 16) * 16
    quarter = jnp.pad(quarter, ((0, 0), (0, 0), (0, r_pad - r_loc), (0, 0)))
    ct = coeffs.reshape(n_mo, r_loc, nmo)
    ct = jnp.pad(ct, ((0, 0), (0, r_pad - r_loc), (0, 0))).reshape(n_mo * r_pad, nmo).T
    return pl.pallas_call(
        functools.partial(fused_kernel, n_pair, n_mo, N_CHUNK),
        out_shape=jax.ShapeDtypeStruct((n_pair * rows, iw, jw), jnp.float32),
        in_specs=[
            pl.BlockSpec(memory_space=pltpu.SMEM),
            pl.BlockSpec(memory_space=pltpu.VMEM),
            pl.BlockSpec(memory_space=pltpu.VMEM),
        ],
        out_specs=pl.BlockSpec(memory_space=pltpu.VMEM),
        scratch_shapes=[
            pltpu.VMEM((rows, n_mo, r_pad, jw), quarter.dtype),
            pltpu.VMEM((rows, n_pair, iw, jw), jnp.bfloat16),
            pltpu.VMEM((n_pair, rows, iw, jw), jnp.bfloat16),
            pltpu.SemaphoreType.DMA((N_CHUNK, n_mo)),
            pltpu.SemaphoreType.DMA((N_CHUNK, n_mo)),
            pltpu.SemaphoreType.DMA((N_CHUNK, n_pair)),
            pltpu.SemaphoreType.DMA((N_CHUNK, n_pair)),
            pltpu.SemaphoreType.DMA((2, N_CHUNK)),
        ],
        compiler_params=pltpu.CompilerParams(
            collective_id=0, has_side_effects=True, vmem_limit_bytes=48 * 1024 * 1024
        ),
    )(mirror, quarter, ct)


def make_on_device(n_pair, n_mo):
    def on_device(integrals, coeffs, mirror):
        rows, r_loc, nbf = integrals.shape
        nmo = coeffs.shape[1]
        c_j = coeffs.reshape(nbf, n_mo, nmo // n_mo).transpose(1, 0, 2)
        quarter = jnp.einsum(
            "krs,bsj->bkrj", integrals, c_j, preferred_element_type=jnp.float32
        ).astype(jnp.bfloat16)
        return fused(quarter, coeffs, mirror, n_pair)

    return on_device


def solution(mesh):
    return jax.shard_map(
        make_on_device(mesh.shape["pair"], mesh.shape["mo"]),
        mesh=mesh,
        in_specs=(P("pair", "mo", None), P(), P()),
        out_specs=P(None, "pair", "mo"),
        check_vma=False,
    )
```

```python
import functools

import jax
import jax.numpy as jnp
from jax import lax
from jax.experimental import pallas as pl
from jax.experimental.pallas import tpu as pltpu
from jax.sharding import PartitionSpec as P

MESH = pl.DeviceIdType.MESH
N_CHUNK = 4


def fused_kernel(n_pair, n_mo, n_chunk, mirror_ref, x_ref, c_ref, ct_ref, o_ref,
                 q_ref, arrived, sendbuf, held, mo_send, mo_recv, pr_send, pr_recv, own_sem):
    me = lax.axis_index("pair")
    mo = lax.axis_index("mo")
    rows = q_ref.shape[1]
    kc = rows // n_chunk

    def chunk(c):
        return pl.ds(c * kc, kc)

    def mo_copy(c, s):
        b = lax.rem(mo + s, n_mo)
        return pltpu.make_async_remote_copy(
            src_ref=q_ref.at[b, chunk(c)],
            dst_ref=arrived.at[mo, chunk(c)],
            send_sem=mo_send.at[c, s],
            recv_sem=mo_recv.at[c, s],
            device_id=(me, b),
            device_id_type=MESH,
        )

    def pair_copy(c, s):
        p = lax.rem(me + s, n_pair)
        return pltpu.make_async_remote_copy(
            src_ref=sendbuf.at[chunk(c), p],
            dst_ref=held.at[me, chunk(c)],
            send_sem=pr_send.at[c, s],
            recv_sem=pr_recv.at[c, s],
            device_id=(p, mo),
            device_id_type=MESH,
        )

    def own_mo(c):
        return pltpu.make_async_copy(q_ref.at[mo, chunk(c)], arrived.at[mo, chunk(c)], own_sem.at[0, c])

    def own_pair(c):
        return pltpu.make_async_copy(sendbuf.at[chunk(c), me], held.at[me, chunk(c)], own_sem.at[1, c])

    barrier = pltpu.get_barrier_semaphore()

    def greet(s, carry):
        pl.semaphore_signal(barrier, 1, device_id=(lax.rem(me + s, n_pair), mo), device_id_type=MESH)
        return carry

    lax.fori_loop(1, n_pair, greet, 0)
    for s in range(1, n_mo):
        pl.semaphore_signal(barrier, 1, device_id=(me, lax.rem(mo + s, n_mo)), device_id_type=MESH)
    pl.semaphore_wait(barrier, n_pair - 1 + n_mo - 1)

    jw = q_ref.shape[-1]
    for c in range(n_chunk):

        for t in range(kc):
            k = c * kc + t
            res = jnp.dot(x_ref[:, k, :], c_ref[...], preferred_element_type=jnp.float32)
            res = res.astype(q_ref.dtype)
            for b in range(n_mo):
                q_ref[b, k] = res[:, b * jw:(b + 1) * jw]
        own_mo(c).start()
        for s in range(1, n_mo):
            mo_copy(c, s).start()

    for c in range(n_chunk):
        own_mo(c).wait()
        for s in range(1, n_mo):
            mo_copy(c, s).wait()

        def transform(t, carry):
            k = c * kc + t
            acc = jnp.dot(ct_ref[0], arrived[0, k], preferred_element_type=jnp.float32)
            for b in range(1, n_mo):
                acc += jnp.dot(ct_ref[b], arrived[b, k], preferred_element_type=jnp.float32)
            sendbuf[k] = acc.reshape(n_pair, -1, acc.shape[-1]).astype(sendbuf.dtype)
            return carry

        lax.fori_loop(0, kc, transform, 0)
        own_pair(c).start()

        def start(s, carry):
            pair_copy(c, s).start()
            return carry

        lax.fori_loop(1, n_pair, start, 0)

    for c in range(n_chunk):
        own_pair(c).wait()

        def finish(s, carry):
            pair_copy(c, s).wait()
            return carry

        lax.fori_loop(1, n_pair, finish, 0)

    def combine(src, carry):
        for kk in range(rows):
            k = src * rows + kk
            m = mirror_ref[k]
            a = held[src, kk].astype(jnp.float32)
            b = held[m // rows, m % rows].astype(jnp.float32)
            o_ref[k] = 0.5 * (a + b)
        return carry

    lax.fori_loop(0, n_pair, combine, 0)


def fused(integrals, coeffs, ct, mirror, n_pair, n_mo):
    rows, r_loc, _ = integrals.shape
    integrals = integrals.transpose(1, 0, 2)
    nmo = coeffs.shape[1]
    iw, jw = nmo // n_pair, nmo // n_mo
    return pl.pallas_call(
        functools.partial(fused_kernel, n_pair, n_mo, N_CHUNK),
        out_shape=jax.ShapeDtypeStruct((n_pair * rows, iw, jw), jnp.float32),
        in_specs=[pl.BlockSpec(memory_space=pltpu.SMEM)]
        + [pl.BlockSpec(memory_space=pltpu.VMEM)] * 3,
        out_specs=pl.BlockSpec(memory_space=pltpu.VMEM),
        scratch_shapes=[
            pltpu.VMEM((n_mo, rows, r_loc, jw), jnp.bfloat16),
            pltpu.VMEM((n_mo, rows, r_loc, jw), jnp.bfloat16),
            pltpu.VMEM((rows, n_pair, iw, jw), jnp.bfloat16),
            pltpu.VMEM((n_pair, rows, iw, jw), jnp.bfloat16),
            pltpu.SemaphoreType.DMA((N_CHUNK, n_mo)),
            pltpu.SemaphoreType.DMA((N_CHUNK, n_mo)),
            pltpu.SemaphoreType.DMA((N_CHUNK, n_pair)),
            pltpu.SemaphoreType.DMA((N_CHUNK, n_pair)),
            pltpu.SemaphoreType.DMA((2, N_CHUNK)),
        ],
        compiler_params=pltpu.CompilerParams(
            collective_id=0, has_side_effects=True, vmem_limit_bytes=60 * 1024 * 1024
        ),
    )(mirror, integrals, coeffs, ct)


def make_on_device(n_pair, n_mo):
    def on_device(integrals, coeffs, mirror):
        rows, r_loc, nbf = integrals.shape
        nmo = coeffs.shape[1]
        ct = coeffs.reshape(n_mo, r_loc, nmo).transpose(0, 2, 1)
        return fused(integrals, coeffs, ct, mirror, n_pair, n_mo)

    return on_device


def solution(mesh):
    return jax.shard_map(
        make_on_device(mesh.shape["pair"], mesh.shape["mo"]),
        mesh=mesh,
        in_specs=(P("pair", "mo", None), P(), P()),
        out_specs=P(None, "pair", "mo"),
        check_vma=False,
    )
```

```python
import functools

import jax
import jax.numpy as jnp
from jax import lax
from jax.experimental import pallas as pl
from jax.experimental.pallas import tpu as pltpu
from jax.sharding import PartitionSpec as P

MESH = pl.DeviceIdType.MESH
N_CHUNK = 4


def fused_kernel(n_pair, n_mo, n_chunk, x_ref, c_ref, ct_ref, held,
                 q_ref, arrived, sendbuf, mo_send, mo_recv, pr_send, pr_recv, own_sem):
    me = lax.axis_index("pair")
    mo = lax.axis_index("mo")
    rows = q_ref.shape[1]
    kc = rows // n_chunk

    def chunk(c):
        return pl.ds(c * kc, kc)

    def mo_copy(c, s):
        b = lax.rem(mo + s, n_mo)
        return pltpu.make_async_remote_copy(
            src_ref=q_ref.at[b, chunk(c)],
            dst_ref=arrived.at[mo, chunk(c)],
            send_sem=mo_send.at[c, s],
            recv_sem=mo_recv.at[c, s],
            device_id=(me, b),
            device_id_type=MESH,
        )

    def pair_copy(c, s):
        p = lax.rem(me + s, n_pair)
        return pltpu.make_async_remote_copy(
            src_ref=sendbuf.at[chunk(c), p],
            dst_ref=held.at[me, chunk(c)],
            send_sem=pr_send.at[c, s],
            recv_sem=pr_recv.at[c, s],
            device_id=(p, mo),
            device_id_type=MESH,
        )

    def own_mo(c):
        return pltpu.make_async_copy(q_ref.at[mo, chunk(c)], arrived.at[mo, chunk(c)], own_sem.at[0, c])

    def own_pair(c):
        return pltpu.make_async_copy(sendbuf.at[chunk(c), me], held.at[me, chunk(c)], own_sem.at[1, c])

    barrier = pltpu.get_barrier_semaphore()

    def greet(s, carry):
        pl.semaphore_signal(barrier, 1, device_id=(lax.rem(me + s, n_pair), mo), device_id_type=MESH)
        return carry

    lax.fori_loop(1, n_pair, greet, 0)
    for s in range(1, n_mo):
        pl.semaphore_signal(barrier, 1, device_id=(me, lax.rem(mo + s, n_mo)), device_id_type=MESH)
    pl.semaphore_wait(barrier, n_pair - 1 + n_mo - 1)

    jw = q_ref.shape[-1]
    for c in range(n_chunk):

        for t in range(kc):
            k = c * kc + t
            res = jnp.dot(x_ref[:, k, :], c_ref[...], preferred_element_type=jnp.float32)
            res = res.astype(q_ref.dtype)
            for b in range(n_mo):
                q_ref[b, k] = res[:, b * jw:(b + 1) * jw]
        own_mo(c).start()
        for s in range(1, n_mo):
            mo_copy(c, s).start()

    for c in range(n_chunk):
        own_mo(c).wait()
        for s in range(1, n_mo):
            mo_copy(c, s).wait()

        def transform(t, carry):
            k = c * kc + t
            acc = jnp.dot(ct_ref[0], arrived[0, k], preferred_element_type=jnp.float32)
            for b in range(1, n_mo):
                acc += jnp.dot(ct_ref[b], arrived[b, k], preferred_element_type=jnp.float32)
            sendbuf[k] = acc.reshape(n_pair, -1, acc.shape[-1]).astype(sendbuf.dtype)
            return carry

        lax.fori_loop(0, kc, transform, 0)
        own_pair(c).start()

        def start(s, carry):
            pair_copy(c, s).start()
            return carry

        lax.fori_loop(1, n_pair, start, 0)

    for c in range(n_chunk):
        own_pair(c).wait()

        def finish(s, carry):
            pair_copy(c, s).wait()
            return carry

        lax.fori_loop(1, n_pair, finish, 0)


def fused(integrals, coeffs, ct, n_pair, n_mo):
    rows, r_loc, _ = integrals.shape
    integrals = integrals.transpose(1, 0, 2)
    nmo = coeffs.shape[1]
    iw, jw = nmo // n_pair, nmo // n_mo
    return pl.pallas_call(
        functools.partial(fused_kernel, n_pair, n_mo, N_CHUNK),
        out_shape=jax.ShapeDtypeStruct((n_pair, rows, iw, jw), jnp.bfloat16),
        in_specs=[pl.BlockSpec(memory_space=pltpu.VMEM)] * 3,
        out_specs=pl.BlockSpec(memory_space=pltpu.VMEM),
        scratch_shapes=[
            pltpu.VMEM((n_mo, rows, r_loc, jw), jnp.bfloat16),
            pltpu.VMEM((n_mo, rows, r_loc, jw), jnp.bfloat16),
            pltpu.VMEM((rows, n_pair, iw, jw), jnp.bfloat16),
            pltpu.SemaphoreType.DMA((N_CHUNK, n_mo)),
            pltpu.SemaphoreType.DMA((N_CHUNK, n_mo)),
            pltpu.SemaphoreType.DMA((N_CHUNK, n_pair)),
            pltpu.SemaphoreType.DMA((N_CHUNK, n_pair)),
            pltpu.SemaphoreType.DMA((2, N_CHUNK)),
        ],
        compiler_params=pltpu.CompilerParams(
            collective_id=0, has_side_effects=True, vmem_limit_bytes=60 * 1024 * 1024
        ),
    )(integrals, coeffs, ct)


def combine_kernel(mirror_ref, x_ref, o_ref):
    def body(k, carry):
        a = x_ref[k].astype(jnp.float32)
        b = x_ref[mirror_ref[k]].astype(jnp.float32)
        o_ref[k] = 0.5 * (a + b)
        return carry

    lax.fori_loop(0, x_ref.shape[0], body, 0, unroll=8)


def combine(pieces, mirror):
    return pl.pallas_call(
        combine_kernel,
        out_shape=jax.ShapeDtypeStruct(pieces.shape, jnp.float32),
        in_specs=[
            pl.BlockSpec(memory_space=pltpu.SMEM),
            pl.BlockSpec(memory_space=pltpu.VMEM),
        ],
        out_specs=pl.BlockSpec(memory_space=pltpu.VMEM),
    )(mirror, pieces)


def make_on_device(n_pair, n_mo):
    def on_device(integrals, coeffs, mirror):
        rows, r_loc, nbf = integrals.shape
        nmo = coeffs.shape[1]
        ct = coeffs.reshape(n_mo, r_loc, nmo).transpose(0, 2, 1)
        held = fused(integrals, coeffs, ct, n_pair, n_mo)
        return combine(held.reshape(-1, *held.shape[2:]), mirror)

    return on_device


def solution(mesh):
    return jax.shard_map(
        make_on_device(mesh.shape["pair"], mesh.shape["mo"]),
        mesh=mesh,
        in_specs=(P("pair", "mo", None), P(), P()),
        out_specs=P(None, "pair", "mo"),
        check_vma=False,
    )
```

```python
import functools

import jax
import jax.numpy as jnp
from jax import lax
from jax.experimental import pallas as pl
from jax.experimental.pallas import tpu as pltpu
from jax.sharding import PartitionSpec as P

MESH = pl.DeviceIdType.MESH
N_CHUNK = 4


def fused_kernel(n_pair, n_mo, n_chunk, x_ref, c_ref, ct_ref, held,
                 q_ref, arrived, sendbuf, mo_send, mo_recv, pr_send, pr_recv, own_sem):
    me = lax.axis_index("pair")
    mo = lax.axis_index("mo")
    rows = q_ref.shape[1]
    kc = rows // n_chunk

    def chunk(c):
        return pl.ds(c * kc, kc)

    def mo_copy(c, s):
        b = lax.rem(mo + s, n_mo)
        return pltpu.make_async_remote_copy(
            src_ref=q_ref.at[b, chunk(c)],
            dst_ref=arrived.at[mo, chunk(c)],
            send_sem=mo_send.at[c, s],
            recv_sem=mo_recv.at[c, s],
            device_id=(me, b),
            device_id_type=MESH,
        )

    def pair_copy(c, s):
        p = lax.rem(me + s, n_pair)
        return pltpu.make_async_remote_copy(
            src_ref=sendbuf.at[chunk(c), p],
            dst_ref=held.at[me, chunk(c)],
            send_sem=pr_send.at[c, s],
            recv_sem=pr_recv.at[c, s],
            device_id=(p, mo),
            device_id_type=MESH,
        )

    def own_mo(c):
        return pltpu.make_async_copy(q_ref.at[mo, chunk(c)], arrived.at[mo, chunk(c)], own_sem.at[0, c])

    def own_pair(c):
        return pltpu.make_async_copy(sendbuf.at[chunk(c), me], held.at[me, chunk(c)], own_sem.at[1, c])

    barrier = pltpu.get_barrier_semaphore()

    def greet(s, carry):
        pl.semaphore_signal(barrier, 1, device_id=(lax.rem(me + s, n_pair), mo), device_id_type=MESH)
        return carry

    lax.fori_loop(1, n_pair, greet, 0)
    for s in range(1, n_mo):
        pl.semaphore_signal(barrier, 1, device_id=(me, lax.rem(mo + s, n_mo)), device_id_type=MESH)

    jw = q_ref.shape[-1]
    for c in range(n_chunk):

        for t in range(kc):
            k = c * kc + t
            res = jnp.dot(x_ref[:, k, :], c_ref[...], preferred_element_type=jnp.float32)
            res = res.astype(q_ref.dtype)
            for b in range(n_mo):
                q_ref[b, k] = res[:, b * jw:(b + 1) * jw]
        own_mo(c).start()
        if c == 0:
            pl.semaphore_wait(barrier, n_pair - 1 + n_mo - 1)
        for s in range(1, n_mo):
            mo_copy(c, s).start()

    for c in range(n_chunk):
        own_mo(c).wait()
        for s in range(1, n_mo):
            mo_copy(c, s).wait()

        def transform(t, carry):
            k = c * kc + t
            acc = jnp.dot(ct_ref[0], arrived[0, k], preferred_element_type=jnp.float32)
            for b in range(1, n_mo):
                acc += jnp.dot(ct_ref[b], arrived[b, k], preferred_element_type=jnp.float32)
            sendbuf[k] = acc.reshape(n_pair, -1, acc.shape[-1]).astype(sendbuf.dtype)
            return carry

        lax.fori_loop(0, kc, transform, 0)
        own_pair(c).start()

        def start(s, carry):
            pair_copy(c, s).start()
            return carry

        lax.fori_loop(1, n_pair, start, 0)

    for c in range(n_chunk):
        own_pair(c).wait()

        def finish(s, carry):
            pair_copy(c, s).wait()
            return carry

        lax.fori_loop(1, n_pair, finish, 0)


def fused(integrals, coeffs, ct, n_pair, n_mo):
    rows, r_loc, _ = integrals.shape
    integrals = integrals.transpose(1, 0, 2)
    nmo = coeffs.shape[1]
    iw, jw = nmo // n_pair, nmo // n_mo
    return pl.pallas_call(
        functools.partial(fused_kernel, n_pair, n_mo, N_CHUNK),
        out_shape=jax.ShapeDtypeStruct((n_pair, rows, iw, jw), jnp.bfloat16),
        in_specs=[pl.BlockSpec(memory_space=pltpu.VMEM)] * 3,
        out_specs=pl.BlockSpec(memory_space=pltpu.VMEM),
        scratch_shapes=[
            pltpu.VMEM((n_mo, rows, r_loc, jw), jnp.bfloat16),
            pltpu.VMEM((n_mo, rows, r_loc, jw), jnp.bfloat16),
            pltpu.VMEM((rows, n_pair, iw, jw), jnp.bfloat16),
            pltpu.SemaphoreType.DMA((N_CHUNK, n_mo)),
            pltpu.SemaphoreType.DMA((N_CHUNK, n_mo)),
            pltpu.SemaphoreType.DMA((N_CHUNK, n_pair)),
            pltpu.SemaphoreType.DMA((N_CHUNK, n_pair)),
            pltpu.SemaphoreType.DMA((2, N_CHUNK)),
        ],
        compiler_params=pltpu.CompilerParams(
            collective_id=0, has_side_effects=True, vmem_limit_bytes=60 * 1024 * 1024
        ),
    )(integrals, coeffs, ct)


def combine_kernel(mirror_ref, x_ref, o_ref):
    def body(k, carry):
        a = x_ref[k].astype(jnp.float32)
        b = x_ref[mirror_ref[k]].astype(jnp.float32)
        o_ref[k] = 0.5 * (a + b)
        return carry

    lax.fori_loop(0, x_ref.shape[0], body, 0, unroll=8)


def combine(pieces, mirror):
    return pl.pallas_call(
        combine_kernel,
        out_shape=jax.ShapeDtypeStruct(pieces.shape, jnp.float32),
        in_specs=[
            pl.BlockSpec(memory_space=pltpu.SMEM),
            pl.BlockSpec(memory_space=pltpu.VMEM),
        ],
        out_specs=pl.BlockSpec(memory_space=pltpu.VMEM),
    )(mirror, pieces)


def make_on_device(n_pair, n_mo):
    def on_device(integrals, coeffs, mirror):
        rows, r_loc, nbf = integrals.shape
        nmo = coeffs.shape[1]
        ct = coeffs.reshape(n_mo, r_loc, nmo).transpose(0, 2, 1)
        held = fused(integrals, coeffs, ct, n_pair, n_mo)
        return combine(held.reshape(-1, *held.shape[2:]), mirror)

    return on_device


def solution(mesh):
    return jax.shard_map(
        make_on_device(mesh.shape["pair"], mesh.shape["mo"]),
        mesh=mesh,
        in_specs=(P("pair", "mo", None), P(), P()),
        out_specs=P(None, "pair", "mo"),
        check_vma=False,
    )
```

```python
import functools

import jax
import jax.numpy as jnp
from jax import lax
from jax.experimental import pallas as pl
from jax.experimental.pallas import tpu as pltpu
from jax.sharding import PartitionSpec as P

MESH = pl.DeviceIdType.MESH
N_CHUNK = 8


def fused_kernel(n_pair, n_mo, n_chunk, x_ref, c_ref, ct_ref, held,
                 q_ref, arrived, sendbuf, mo_send, mo_recv, pr_send, pr_recv, own_sem):
    me = lax.axis_index("pair")
    mo = lax.axis_index("mo")
    rows = q_ref.shape[1]
    kc = rows // n_chunk

    def chunk(c):
        return pl.ds(c * kc, kc)

    def mo_copy(c, s):
        b = lax.rem(mo + s, n_mo)
        return pltpu.make_async_remote_copy(
            src_ref=q_ref.at[b, chunk(c)],
            dst_ref=arrived.at[mo, chunk(c)],
            send_sem=mo_send.at[c, s],
            recv_sem=mo_recv.at[c, s],
            device_id=(me, b),
            device_id_type=MESH,
        )

    def pair_copy(c, s):
        p = lax.rem(me + s, n_pair)
        return pltpu.make_async_remote_copy(
            src_ref=sendbuf.at[chunk(c), p],
            dst_ref=held.at[me, chunk(c)],
            send_sem=pr_send.at[c, s],
            recv_sem=pr_recv.at[c, s],
            device_id=(p, mo),
            device_id_type=MESH,
        )

    def own_mo(c):
        return pltpu.make_async_copy(q_ref.at[mo, chunk(c)], arrived.at[mo, chunk(c)], own_sem.at[0, c])

    def own_pair(c):
        return pltpu.make_async_copy(sendbuf.at[chunk(c), me], held.at[me, chunk(c)], own_sem.at[1, c])

    barrier = pltpu.get_barrier_semaphore()

    def greet(s, carry):
        pl.semaphore_signal(barrier, 1, device_id=(lax.rem(me + s, n_pair), mo), device_id_type=MESH)
        return carry

    lax.fori_loop(1, n_pair, greet, 0)
    for s in range(1, n_mo):
        pl.semaphore_signal(barrier, 1, device_id=(me, lax.rem(mo + s, n_mo)), device_id_type=MESH)

    jw = q_ref.shape[-1]
    for c in range(n_chunk):

        for t in range(kc):
            k = c * kc + t
            res = jnp.dot(x_ref[:, k, :], c_ref[...], preferred_element_type=jnp.float32)
            res = res.astype(q_ref.dtype)
            for b in range(n_mo):
                q_ref[b, k] = res[:, b * jw:(b + 1) * jw]
        own_mo(c).start()
        if c == 0:
            pl.semaphore_wait(barrier, n_pair - 1 + n_mo - 1)
        for s in range(1, n_mo):
            mo_copy(c, s).start()

    for c in range(n_chunk):
        own_mo(c).wait()
        for s in range(1, n_mo):
            mo_copy(c, s).wait()

        def transform(t, carry):
            k = c * kc + t
            acc = jnp.dot(ct_ref[0], arrived[0, k], preferred_element_type=jnp.float32)
            for b in range(1, n_mo):
                acc += jnp.dot(ct_ref[b], arrived[b, k], preferred_element_type=jnp.float32)
            sendbuf[k] = acc.reshape(n_pair, -1, acc.shape[-1]).astype(sendbuf.dtype)
            return carry

        lax.fori_loop(0, kc, transform, 0)
        own_pair(c).start()

        def start(s, carry):
            pair_copy(c, s).start()
            return carry

        lax.fori_loop(1, n_pair, start, 0)

    for c in range(n_chunk):
        own_pair(c).wait()

        def finish(s, carry):
            pair_copy(c, s).wait()
            return carry

        lax.fori_loop(1, n_pair, finish, 0)


def fused(integrals, coeffs, ct, n_pair, n_mo):
    rows, r_loc, _ = integrals.shape
    integrals = integrals.transpose(1, 0, 2)
    nmo = coeffs.shape[1]
    iw, jw = nmo // n_pair, nmo // n_mo
    return pl.pallas_call(
        functools.partial(fused_kernel, n_pair, n_mo, N_CHUNK),
        out_shape=jax.ShapeDtypeStruct((n_pair, rows, iw, jw), jnp.bfloat16),
        in_specs=[pl.BlockSpec(memory_space=pltpu.VMEM)] * 3,
        out_specs=pl.BlockSpec(memory_space=pltpu.VMEM),
        scratch_shapes=[
            pltpu.VMEM((n_mo, rows, r_loc, jw), jnp.bfloat16),
            pltpu.VMEM((n_mo, rows, r_loc, jw), jnp.bfloat16),
            pltpu.VMEM((rows, n_pair, iw, jw), jnp.bfloat16),
            pltpu.SemaphoreType.DMA((N_CHUNK, n_mo)),
            pltpu.SemaphoreType.DMA((N_CHUNK, n_mo)),
            pltpu.SemaphoreType.DMA((N_CHUNK, n_pair)),
            pltpu.SemaphoreType.DMA((N_CHUNK, n_pair)),
            pltpu.SemaphoreType.DMA((2, N_CHUNK)),
        ],
        compiler_params=pltpu.CompilerParams(
            collective_id=0, has_side_effects=True, vmem_limit_bytes=60 * 1024 * 1024
        ),
    )(integrals, coeffs, ct)


def combine_kernel(mirror_ref, x_ref, o_ref):
    def body(k, carry):
        a = x_ref[k].astype(jnp.float32)
        b = x_ref[mirror_ref[k]].astype(jnp.float32)
        o_ref[k] = 0.5 * (a + b)
        return carry

    lax.fori_loop(0, x_ref.shape[0], body, 0, unroll=8)


def combine(pieces, mirror):
    return pl.pallas_call(
        combine_kernel,
        out_shape=jax.ShapeDtypeStruct(pieces.shape, jnp.float32),
        in_specs=[
            pl.BlockSpec(memory_space=pltpu.SMEM),
            pl.BlockSpec(memory_space=pltpu.VMEM),
        ],
        out_specs=pl.BlockSpec(memory_space=pltpu.VMEM),
    )(mirror, pieces)


def make_on_device(n_pair, n_mo):
    def on_device(integrals, coeffs, mirror):
        rows, r_loc, nbf = integrals.shape
        nmo = coeffs.shape[1]
        ct = coeffs.reshape(n_mo, r_loc, nmo).transpose(0, 2, 1)
        held = fused(integrals, coeffs, ct, n_pair, n_mo)
        return combine(held.reshape(-1, *held.shape[2:]), mirror)

    return on_device


def solution(mesh):
    return jax.shard_map(
        make_on_device(mesh.shape["pair"], mesh.shape["mo"]),
        mesh=mesh,
        in_specs=(P("pair", "mo", None), P(), P()),
        out_specs=P(None, "pair", "mo"),
        check_vma=False,
    )
```

```python
import functools

import jax
import jax.numpy as jnp
from jax import lax
from jax.experimental import pallas as pl
from jax.experimental.pallas import tpu as pltpu
from jax.sharding import PartitionSpec as P

MESH = pl.DeviceIdType.MESH
N_CHUNK = 4


def fused_kernel(n_pair, n_mo, n_chunk, x_ref, c_ref, ct_ref, held,
                 q_ref, arrived, sendbuf, mo_send, mo_recv, pr_send, pr_recv, own_sem):
    me = lax.axis_index("pair")
    mo = lax.axis_index("mo")
    rows = q_ref.shape[1]
    kc = rows // n_chunk

    def chunk(c):
        return pl.ds(c * kc, kc)

    def mo_copy(c, s):
        b = lax.rem(mo + s, n_mo)
        return pltpu.make_async_remote_copy(
            src_ref=q_ref.at[b, chunk(c)],
            dst_ref=arrived.at[mo, chunk(c)],
            send_sem=mo_send.at[c, s],
            recv_sem=mo_recv.at[c, s],
            device_id=(me, b),
            device_id_type=MESH,
        )

    def pair_copy(c, s):
        p = lax.rem(me + s, n_pair)
        return pltpu.make_async_remote_copy(
            src_ref=sendbuf.at[chunk(c), p],
            dst_ref=held.at[me, chunk(c)],
            send_sem=pr_send.at[c, s],
            recv_sem=pr_recv.at[c, s],
            device_id=(p, mo),
            device_id_type=MESH,
        )

    def own_mo(c):
        return pltpu.make_async_copy(q_ref.at[mo, chunk(c)], arrived.at[mo, chunk(c)], own_sem.at[0, c])

    def own_pair(c):
        return pltpu.make_async_copy(sendbuf.at[chunk(c), me], held.at[me, chunk(c)], own_sem.at[1, c])

    barrier = pltpu.get_barrier_semaphore()

    def greet(s, carry):
        pl.semaphore_signal(barrier, 1, device_id=(lax.rem(me + s, n_pair), mo), device_id_type=MESH)
        return carry

    lax.fori_loop(1, n_pair, greet, 0)
    for s in range(1, n_mo):
        pl.semaphore_signal(barrier, 1, device_id=(me, lax.rem(mo + s, n_mo)), device_id_type=MESH)

    jw = q_ref.shape[-1]
    for c in range(n_chunk):

        for t in range(kc):
            k = c * kc + t
            res = jnp.dot(x_ref[:, k, :], c_ref[...], preferred_element_type=jnp.float32)
            res = res.astype(q_ref.dtype)
            for b in range(n_mo):
                q_ref[b, k] = res[:, b * jw:(b + 1) * jw]
        own_mo(c).start()
        if c == 0:
            pl.semaphore_wait(barrier, n_pair - 1 + n_mo - 1)
        for s in range(1, n_mo):
            mo_copy(c, s).start()

    for c in range(n_chunk):
        own_mo(c).wait()
        for s in range(1, n_mo):
            mo_copy(c, s).wait()

        def transform(t, carry):
            k = c * kc + t
            r_loc = arrived.shape[2]
            acc = jnp.dot(ct_ref[:, 0:r_loc], arrived[0, k], preferred_element_type=jnp.float32)
            for b in range(1, n_mo):
                cols = ct_ref[:, b * r_loc:(b + 1) * r_loc]
                acc += jnp.dot(cols, arrived[b, k], preferred_element_type=jnp.float32)
            sendbuf[k] = acc.reshape(n_pair, -1, acc.shape[-1]).astype(sendbuf.dtype)
            return carry

        lax.fori_loop(0, kc, transform, 0)
        own_pair(c).start()

        def start(s, carry):
            pair_copy(c, s).start()
            return carry

        lax.fori_loop(1, n_pair, start, 0)

    for c in range(n_chunk):
        own_pair(c).wait()

        def finish(s, carry):
            pair_copy(c, s).wait()
            return carry

        lax.fori_loop(1, n_pair, finish, 0)


def fused(integrals, coeffs, ct, n_pair, n_mo):
    rows, r_loc, _ = integrals.shape
    integrals = integrals.transpose(1, 0, 2)
    nmo = coeffs.shape[1]
    iw, jw = nmo // n_pair, nmo // n_mo
    return pl.pallas_call(
        functools.partial(fused_kernel, n_pair, n_mo, N_CHUNK),
        out_shape=jax.ShapeDtypeStruct((n_pair, rows, iw, jw), jnp.bfloat16),
        in_specs=[pl.BlockSpec(memory_space=pltpu.VMEM)] * 3,
        out_specs=pl.BlockSpec(memory_space=pltpu.VMEM),
        scratch_shapes=[
            pltpu.VMEM((n_mo, rows, r_loc, jw), jnp.bfloat16),
            pltpu.VMEM((n_mo, rows, r_loc, jw), jnp.bfloat16),
            pltpu.VMEM((rows, n_pair, iw, jw), jnp.bfloat16),
            pltpu.SemaphoreType.DMA((N_CHUNK, n_mo)),
            pltpu.SemaphoreType.DMA((N_CHUNK, n_mo)),
            pltpu.SemaphoreType.DMA((N_CHUNK, n_pair)),
            pltpu.SemaphoreType.DMA((N_CHUNK, n_pair)),
            pltpu.SemaphoreType.DMA((2, N_CHUNK)),
        ],
        compiler_params=pltpu.CompilerParams(
            collective_id=0, has_side_effects=True, vmem_limit_bytes=60 * 1024 * 1024
        ),
    )(integrals, coeffs, ct)


def combine_kernel(mirror_ref, x_ref, o_ref):
    def body(k, carry):
        a = x_ref[k].astype(jnp.float32)
        b = x_ref[mirror_ref[k]].astype(jnp.float32)
        o_ref[k] = 0.5 * (a + b)
        return carry

    lax.fori_loop(0, x_ref.shape[0], body, 0, unroll=8)


def combine(pieces, mirror):
    return pl.pallas_call(
        combine_kernel,
        out_shape=jax.ShapeDtypeStruct(pieces.shape, jnp.float32),
        in_specs=[
            pl.BlockSpec(memory_space=pltpu.SMEM),
            pl.BlockSpec(memory_space=pltpu.VMEM),
        ],
        out_specs=pl.BlockSpec(memory_space=pltpu.VMEM),
    )(mirror, pieces)


def make_on_device(n_pair, n_mo):
    def on_device(integrals, coeffs, mirror):
        rows, r_loc, nbf = integrals.shape
        nmo = coeffs.shape[1]
        ct = coeffs.T
        held = fused(integrals, coeffs, ct, n_pair, n_mo)
        return combine(held.reshape(-1, *held.shape[2:]), mirror)

    return on_device


def solution(mesh):
    return jax.shard_map(
        make_on_device(mesh.shape["pair"], mesh.shape["mo"]),
        mesh=mesh,
        in_specs=(P("pair", "mo", None), P(), P()),
        out_specs=P(None, "pair", "mo"),
        check_vma=False,
    )
```

```python
import functools

import jax
import jax.numpy as jnp
from jax import lax
from jax.experimental import pallas as pl
from jax.experimental.pallas import tpu as pltpu
from jax.sharding import PartitionSpec as P

MESH = pl.DeviceIdType.MESH
N_CHUNK = 4


def fused_kernel(n_pair, n_mo, n_chunk, x_ref, c_ref, ct_ref, held,
                 q_ref, arrived, sendbuf, mo_send, mo_recv, pr_send, pr_recv, own_sem):
    me = lax.axis_index("pair")
    mo = lax.axis_index("mo")
    rows = q_ref.shape[1]
    kc = rows // n_chunk

    def chunk(c):
        return pl.ds(c * kc, kc)

    def mo_copy(c, s):
        b = lax.rem(mo + s, n_mo)
        return pltpu.make_async_remote_copy(
            src_ref=q_ref.at[b, chunk(c)],
            dst_ref=arrived.at[mo, chunk(c)],
            send_sem=mo_send.at[c, s],
            recv_sem=mo_recv.at[c, s],
            device_id=(me, b),
            device_id_type=MESH,
        )

    def pair_copy(c, s):
        p = lax.rem(me + s, n_pair)
        return pltpu.make_async_remote_copy(
            src_ref=sendbuf.at[chunk(c), p],
            dst_ref=held.at[me, chunk(c)],
            send_sem=pr_send.at[c, s],
            recv_sem=pr_recv.at[c, s],
            device_id=(p, mo),
            device_id_type=MESH,
        )

    def own_mo(c):
        return pltpu.make_async_copy(q_ref.at[mo, chunk(c)], arrived.at[mo, chunk(c)], own_sem.at[0, c])

    def own_pair(c):
        return pltpu.make_async_copy(sendbuf.at[chunk(c), me], held.at[me, chunk(c)], own_sem.at[1, c])

    barrier = pltpu.get_barrier_semaphore()

    def greet(s, carry):
        pl.semaphore_signal(barrier, 1, device_id=(lax.rem(me + s, n_pair), mo), device_id_type=MESH)
        return carry

    lax.fori_loop(1, n_pair, greet, 0)
    for s in range(1, n_mo):
        pl.semaphore_signal(barrier, 1, device_id=(me, lax.rem(mo + s, n_mo)), device_id_type=MESH)

    jw = q_ref.shape[-1]
    for c in range(n_chunk):

        for t in range(kc):
            k = c * kc + t
            res = jnp.dot(x_ref[:, k, :], c_ref[...], preferred_element_type=jnp.float32)
            res = res.astype(q_ref.dtype)
            for b in range(n_mo):
                q_ref[b, k] = res[:, b * jw:(b + 1) * jw]
        own_mo(c).start()
        if c == 0:
            pl.semaphore_wait(barrier, n_pair - 1 + n_mo - 1)
        for s in range(1, n_mo):
            mo_copy(c, s).start()

    for c in range(n_chunk):
        own_mo(c).wait()
        for s in range(1, n_mo):
            mo_copy(c, s).wait()

        def transform(t, carry):
            k = c * kc + t
            acc = jnp.dot(ct_ref[0], arrived[0, k], preferred_element_type=jnp.float32)
            for b in range(1, n_mo):
                acc += jnp.dot(ct_ref[b], arrived[b, k], preferred_element_type=jnp.float32)
            sendbuf[k] = acc.reshape(n_pair, -1, acc.shape[-1]).astype(sendbuf.dtype)
            return carry

        lax.fori_loop(0, kc, transform, 0)
        own_pair(c).start()

        def start(s, carry):
            pair_copy(c, s).start()
            return carry

        lax.fori_loop(1, n_pair, start, 0)

    for c in range(n_chunk):
        own_pair(c).wait()

        def finish(s, carry):
            pair_copy(c, s).wait()
            return carry

        lax.fori_loop(1, n_pair, finish, 0)


def fused(integrals, coeffs, ct, n_pair, n_mo):
    rows, r_loc, _ = integrals.shape
    integrals = integrals.transpose(1, 0, 2)
    nmo = coeffs.shape[1]
    iw, jw = nmo // n_pair, nmo // n_mo
    return pl.pallas_call(
        functools.partial(fused_kernel, n_pair, n_mo, N_CHUNK),
        out_shape=jax.ShapeDtypeStruct((n_pair, rows, iw, jw), jnp.bfloat16),
        in_specs=[pl.BlockSpec(memory_space=pltpu.VMEM)] * 3,
        out_specs=pl.BlockSpec(memory_space=pltpu.VMEM),
        scratch_shapes=[
            pltpu.VMEM((n_mo, rows, r_loc, jw), jnp.bfloat16),
            pltpu.VMEM((n_mo, rows, r_loc, jw), jnp.bfloat16),
            pltpu.VMEM((rows, n_pair, iw, jw), jnp.bfloat16),
            pltpu.SemaphoreType.DMA((N_CHUNK, n_mo)),
            pltpu.SemaphoreType.DMA((N_CHUNK, n_mo)),
            pltpu.SemaphoreType.DMA((N_CHUNK, n_pair)),
            pltpu.SemaphoreType.DMA((N_CHUNK, n_pair)),
            pltpu.SemaphoreType.DMA((2, N_CHUNK)),
        ],
        compiler_params=pltpu.CompilerParams(
            collective_id=0, has_side_effects=True, vmem_limit_bytes=60 * 1024 * 1024
        ),
    )(integrals, coeffs, ct)


def combine_kernel(mirror_ref, x_ref, o_ref):
    step = 16

    def body(g, carry):
        k0 = pl.multiple_of(g * step, step)
        a = x_ref[pl.ds(k0, step)].astype(jnp.float32)
        b = jnp.stack([x_ref[mirror_ref[k0 + t]] for t in range(step)])
        o_ref[pl.ds(k0, step)] = 0.5 * (a + b.astype(jnp.float32))
        return carry

    lax.fori_loop(0, x_ref.shape[0] // step, body, 0)


def combine(pieces, mirror):
    return pl.pallas_call(
        combine_kernel,
        out_shape=jax.ShapeDtypeStruct(pieces.shape, jnp.float32),
        in_specs=[
            pl.BlockSpec(memory_space=pltpu.SMEM),
            pl.BlockSpec(memory_space=pltpu.VMEM),
        ],
        out_specs=pl.BlockSpec(memory_space=pltpu.VMEM),
    )(mirror, pieces)


def make_on_device(n_pair, n_mo):
    def on_device(integrals, coeffs, mirror):
        rows, r_loc, nbf = integrals.shape
        nmo = coeffs.shape[1]
        ct = coeffs.reshape(n_mo, r_loc, nmo).transpose(0, 2, 1)
        held = fused(integrals, coeffs, ct, n_pair, n_mo)
        return combine(held.reshape(-1, *held.shape[2:]), mirror)

    return on_device


def solution(mesh):
    return jax.shard_map(
        make_on_device(mesh.shape["pair"], mesh.shape["mo"]),
        mesh=mesh,
        in_specs=(P("pair", "mo", None), P(), P()),
        out_specs=P(None, "pair", "mo"),
        check_vma=False,
    )
```

```python
import functools

import jax
import jax.numpy as jnp
from jax import lax
from jax.experimental import pallas as pl
from jax.experimental.pallas import tpu as pltpu
from jax.sharding import PartitionSpec as P

MESH = pl.DeviceIdType.MESH
N_CHUNK = 2


def fused_kernel(n_pair, n_mo, n_chunk, x_ref, c_ref, ct_ref, held,
                 q_ref, arrived, sendbuf, mo_send, mo_recv, pr_send, pr_recv, own_sem):
    me = lax.axis_index("pair")
    mo = lax.axis_index("mo")
    rows = q_ref.shape[1]
    kc = rows // n_chunk

    def chunk(c):
        return pl.ds(c * kc, kc)

    def mo_copy(c, s):
        b = lax.rem(mo + s, n_mo)
        return pltpu.make_async_remote_copy(
            src_ref=q_ref.at[b, chunk(c)],
            dst_ref=arrived.at[mo, chunk(c)],
            send_sem=mo_send.at[c, s],
            recv_sem=mo_recv.at[c, s],
            device_id=(me, b),
            device_id_type=MESH,
        )

    def pair_copy(c, s):
        p = lax.rem(me + s, n_pair)
        return pltpu.make_async_remote_copy(
            src_ref=sendbuf.at[chunk(c), p],
            dst_ref=held.at[me, chunk(c)],
            send_sem=pr_send.at[c, s],
            recv_sem=pr_recv.at[c, s],
            device_id=(p, mo),
            device_id_type=MESH,
        )

    def own_mo(c):
        return pltpu.make_async_copy(q_ref.at[mo, chunk(c)], arrived.at[mo, chunk(c)], own_sem.at[0, c])

    def own_pair(c):
        return pltpu.make_async_copy(sendbuf.at[chunk(c), me], held.at[me, chunk(c)], own_sem.at[1, c])

    barrier = pltpu.get_barrier_semaphore()

    def greet(s, carry):
        pl.semaphore_signal(barrier, 1, device_id=(lax.rem(me + s, n_pair), mo), device_id_type=MESH)
        return carry

    lax.fori_loop(1, n_pair, greet, 0)
    for s in range(1, n_mo):
        pl.semaphore_signal(barrier, 1, device_id=(me, lax.rem(mo + s, n_mo)), device_id_type=MESH)

    jw = q_ref.shape[-1]
    for c in range(n_chunk):

        for t in range(kc):
            k = c * kc + t
            res = jnp.dot(x_ref[:, k, :], c_ref[...], preferred_element_type=jnp.float32)
            res = res.astype(q_ref.dtype)
            for b in range(n_mo):
                q_ref[b, k] = res[:, b * jw:(b + 1) * jw]
        own_mo(c).start()
        if c == 0:
            pl.semaphore_wait(barrier, n_pair - 1 + n_mo - 1)
        for s in range(1, n_mo):
            mo_copy(c, s).start()

    for c in range(n_chunk):
        own_mo(c).wait()
        for s in range(1, n_mo):
            mo_copy(c, s).wait()

        def transform(t, carry):
            k = c * kc + t
            acc = jnp.dot(ct_ref[0], arrived[0, k], preferred_element_type=jnp.float32)
            for b in range(1, n_mo):
                acc += jnp.dot(ct_ref[b], arrived[b, k], preferred_element_type=jnp.float32)
            sendbuf[k] = acc.reshape(n_pair, -1, acc.shape[-1]).astype(sendbuf.dtype)
            return carry

        lax.fori_loop(0, kc, transform, 0)
        own_pair(c).start()

        def start(s, carry):
            pair_copy(c, s).start()
            return carry

        lax.fori_loop(1, n_pair, start, 0)

    for c in range(n_chunk):
        own_pair(c).wait()

        def finish(s, carry):
            pair_copy(c, s).wait()
            return carry

        lax.fori_loop(1, n_pair, finish, 0)


def fused(integrals, coeffs, ct, n_pair, n_mo):
    rows, r_loc, _ = integrals.shape
    integrals = integrals.transpose(1, 0, 2)
    nmo = coeffs.shape[1]
    iw, jw = nmo // n_pair, nmo // n_mo
    return pl.pallas_call(
        functools.partial(fused_kernel, n_pair, n_mo, N_CHUNK),
        out_shape=jax.ShapeDtypeStruct((n_pair, rows, iw, jw), jnp.bfloat16),
        in_specs=[pl.BlockSpec(memory_space=pltpu.VMEM)] * 3,
        out_specs=pl.BlockSpec(memory_space=pltpu.VMEM),
        scratch_shapes=[
            pltpu.VMEM((n_mo, rows, r_loc, jw), jnp.bfloat16),
            pltpu.VMEM((n_mo, rows, r_loc, jw), jnp.bfloat16),
            pltpu.VMEM((rows, n_pair, iw, jw), jnp.bfloat16),
            pltpu.SemaphoreType.DMA((N_CHUNK, n_mo)),
            pltpu.SemaphoreType.DMA((N_CHUNK, n_mo)),
            pltpu.SemaphoreType.DMA((N_CHUNK, n_pair)),
            pltpu.SemaphoreType.DMA((N_CHUNK, n_pair)),
            pltpu.SemaphoreType.DMA((2, N_CHUNK)),
        ],
        compiler_params=pltpu.CompilerParams(
            collective_id=0, has_side_effects=True, vmem_limit_bytes=60 * 1024 * 1024
        ),
    )(integrals, coeffs, ct)


def combine_kernel(mirror_ref, x_ref, o_ref):
    step = 16

    def body(g, carry):
        k0 = pl.multiple_of(g * step, step)
        a = x_ref[pl.ds(k0, step)].astype(jnp.float32)
        b = jnp.stack([x_ref[mirror_ref[k0 + t]] for t in range(step)])
        o_ref[pl.ds(k0, step)] = 0.5 * (a + b.astype(jnp.float32))
        return carry

    lax.fori_loop(0, x_ref.shape[0] // step, body, 0)


def combine(pieces, mirror):
    return pl.pallas_call(
        combine_kernel,
        out_shape=jax.ShapeDtypeStruct(pieces.shape, jnp.float32),
        in_specs=[
            pl.BlockSpec(memory_space=pltpu.SMEM),
            pl.BlockSpec(memory_space=pltpu.VMEM),
        ],
        out_specs=pl.BlockSpec(memory_space=pltpu.VMEM),
    )(mirror, pieces)


def make_on_device(n_pair, n_mo):
    def on_device(integrals, coeffs, mirror):
        rows, r_loc, nbf = integrals.shape
        nmo = coeffs.shape[1]
        ct = coeffs.reshape(n_mo, r_loc, nmo).transpose(0, 2, 1)
        held = fused(integrals, coeffs, ct, n_pair, n_mo)
        return combine(held.reshape(-1, *held.shape[2:]), mirror)

    return on_device


def solution(mesh):
    return jax.shard_map(
        make_on_device(mesh.shape["pair"], mesh.shape["mo"]),
        mesh=mesh,
        in_specs=(P("pair", "mo", None), P(), P()),
        out_specs=P(None, "pair", "mo"),
        check_vma=False,
    )
```

```python
import functools

import jax
import jax.numpy as jnp
from jax import lax
from jax.experimental import pallas as pl
from jax.experimental.pallas import tpu as pltpu
from jax.sharding import PartitionSpec as P

MESH = pl.DeviceIdType.MESH
N_CHUNK = 4


def fused_kernel(n_pair, n_mo, n_chunk, x_ref, c_ref, ct_ref, held,
                 q_ref, arrived, sendbuf, mo_send, mo_recv, pr_send, pr_recv, own_sem):
    me = lax.axis_index("pair")
    mo = lax.axis_index("mo")
    rows = q_ref.shape[1]
    kc = rows // n_chunk

    def chunk(c):
        return pl.ds(c * kc, kc)

    def mo_copy(c, s):
        b = lax.rem(mo + s, n_mo)
        return pltpu.make_async_remote_copy(
            src_ref=q_ref.at[b, chunk(c)],
            dst_ref=arrived.at[mo, chunk(c)],
            send_sem=mo_send.at[c, s],
            recv_sem=mo_recv.at[c, s],
            device_id=(me, b),
            device_id_type=MESH,
        )

    def pair_copy(c, s):
        p = lax.rem(me + s, n_pair)
        return pltpu.make_async_remote_copy(
            src_ref=sendbuf.at[chunk(c), p],
            dst_ref=held.at[me, chunk(c)],
            send_sem=pr_send.at[c, s],
            recv_sem=pr_recv.at[c, s],
            device_id=(p, mo),
            device_id_type=MESH,
        )

    def own_mo(c):
        return pltpu.make_async_copy(q_ref.at[mo, chunk(c)], arrived.at[mo, chunk(c)], own_sem.at[0, c])

    def own_pair(c):
        return pltpu.make_async_copy(sendbuf.at[chunk(c), me], held.at[me, chunk(c)], own_sem.at[1, c])

    barrier = pltpu.get_barrier_semaphore()

    def greet(s, carry):
        pl.semaphore_signal(barrier, 1, device_id=(lax.rem(me + s, n_pair), mo), device_id_type=MESH)
        return carry

    lax.fori_loop(1, n_pair, greet, 0)
    for s in range(1, n_mo):
        pl.semaphore_signal(barrier, 1, device_id=(me, lax.rem(mo + s, n_mo)), device_id_type=MESH)

    jw = q_ref.shape[-1]
    for c in range(n_chunk):

        for t in range(kc):
            k = c * kc + t
            res = jnp.dot(x_ref[:, k, :], c_ref[...], preferred_element_type=jnp.float32)
            res = res.astype(q_ref.dtype)
            for b in range(n_mo):
                q_ref[b, k] = res[:, b * jw:(b + 1) * jw]
        own_mo(c).start()
        if c == 0:
            pl.semaphore_wait(barrier, n_pair - 1 + n_mo - 1)
        for s in range(1, n_mo):
            mo_copy(c, s).start()

    for c in range(n_chunk):
        own_mo(c).wait()
        for s in range(1, n_mo):
            mo_copy(c, s).wait()

        def transform(t, carry):
            k = c * kc + t
            acc = jnp.dot(ct_ref[0], arrived[0, k], preferred_element_type=jnp.float32)
            for b in range(1, n_mo):
                acc += jnp.dot(ct_ref[b], arrived[b, k], preferred_element_type=jnp.float32)
            sendbuf[k] = acc.reshape(n_pair, -1, acc.shape[-1]).astype(sendbuf.dtype)
            return carry

        lax.fori_loop(0, kc, transform, 0)
        own_pair(c).start()

        def start(s, carry):
            pair_copy(c, s).start()
            return carry

        lax.fori_loop(1, n_pair, start, 0)

    for c in range(n_chunk):
        own_pair(c).wait()

        def finish(s, carry):
            pair_copy(c, s).wait()
            return carry

        lax.fori_loop(1, n_pair, finish, 0)


def fused(integrals, coeffs, ct, n_pair, n_mo):
    rows, r_loc, _ = integrals.shape
    integrals = integrals.transpose(1, 0, 2)
    nmo = coeffs.shape[1]
    iw, jw = nmo // n_pair, nmo // n_mo
    return pl.pallas_call(
        functools.partial(fused_kernel, n_pair, n_mo, N_CHUNK),
        out_shape=jax.ShapeDtypeStruct((n_pair, rows, iw, jw), jnp.bfloat16),
        in_specs=[pl.BlockSpec(memory_space=pltpu.VMEM)] * 3,
        out_specs=pl.BlockSpec(memory_space=pltpu.VMEM),
        scratch_shapes=[
            pltpu.VMEM((n_mo, rows, r_loc, jw), jnp.bfloat16),
            pltpu.VMEM((n_mo, rows, r_loc, jw), jnp.bfloat16),
            pltpu.VMEM((rows, n_pair, iw, jw), jnp.bfloat16),
            pltpu.SemaphoreType.DMA((N_CHUNK, n_mo)),
            pltpu.SemaphoreType.DMA((N_CHUNK, n_mo)),
            pltpu.SemaphoreType.DMA((N_CHUNK, n_pair)),
            pltpu.SemaphoreType.DMA((N_CHUNK, n_pair)),
            pltpu.SemaphoreType.DMA((2, N_CHUNK)),
        ],
        compiler_params=pltpu.CompilerParams(
            collective_id=0, has_side_effects=True, vmem_limit_bytes=60 * 1024 * 1024
        ),
    )(integrals, coeffs, ct)


def combine_kernel(mirror_ref, x_ref, o_ref):
    step = 32

    def body(g, carry):
        k0 = pl.multiple_of(g * step, step)
        a = x_ref[pl.ds(k0, step)].astype(jnp.float32)
        b = jnp.stack([x_ref[mirror_ref[k0 + t]] for t in range(step)])
        o_ref[pl.ds(k0, step)] = 0.5 * (a + b.astype(jnp.float32))
        return carry

    lax.fori_loop(0, x_ref.shape[0] // step, body, 0)


def combine(pieces, mirror):
    return pl.pallas_call(
        combine_kernel,
        out_shape=jax.ShapeDtypeStruct(pieces.shape, jnp.float32),
        in_specs=[
            pl.BlockSpec(memory_space=pltpu.SMEM),
            pl.BlockSpec(memory_space=pltpu.VMEM),
        ],
        out_specs=pl.BlockSpec(memory_space=pltpu.VMEM),
    )(mirror, pieces)


def make_on_device(n_pair, n_mo):
    def on_device(integrals, coeffs, mirror):
        rows, r_loc, nbf = integrals.shape
        nmo = coeffs.shape[1]
        ct = coeffs.reshape(n_mo, r_loc, nmo).transpose(0, 2, 1)
        held = fused(integrals, coeffs, ct, n_pair, n_mo)
        return combine(held.reshape(-1, *held.shape[2:]), mirror)

    return on_device


def solution(mesh):
    return jax.shard_map(
        make_on_device(mesh.shape["pair"], mesh.shape["mo"]),
        mesh=mesh,
        in_specs=(P("pair", "mo", None), P(), P()),
        out_specs=P(None, "pair", "mo"),
        check_vma=False,
    )
```
